32 devices in a mesh: gx: 16 (over z, y, core), gy: 2 (over x).
Axes of the slice: x: 2, y: 2, z: 4, core: 2. Of those that a mesh axis runs over, the one named last changes fastest.
Arguments:
- charge: float32 [512, 2048], P('gx', 'gy'), may hold values from -8 to 8
Outputs:
- potential: float32 [512, 2048], P('gx', 'gy')
The draws below stay inside these ranges and needn't reach their ends.
All inputs are finite; a program needn't handle non-finite values.
Results may differ from the reference program's by a relative error of at most 0.0003.
Values sent between devices are 32-bit elements; how exact they have to be, the bound alone decides.
A program may use at most 128 MiB of HBM per device.

```python
import jax
import jax.numpy as jnp
from jax import lax

P_SIZE = 32
W = 16
Q = 4
NL = 16
NX = 512
NY = 64
N_GX = 16
N_GY = 2


def draw_charge(key, part):
    key_values = jax.random.fold_in(key, 0)
    extent = (NX, NY * P_SIZE)
    return jnp.clip(jax.random.normal(key_values, extent, jnp.float32), -8.0, 8.0)


def setup_inputs(seed: int = 0) -> dict:
    streams_of = jax.random.split(jax.random.key(seed), 2)
    return {
        "charge": draw_charge(jax.random.fold_in(streams_of[1], 71), 0),
    }


highest = lax.Precision.HIGHEST

def product(left, right):
    return jnp.matmul(left, right, precision=highest)

def sine_table(length):
    counter = jnp.arange(length, dtype=jnp.int32) + 1
    multiple = counter[:, None] * counter[None, :] % (2 * (length + 1))
    return jnp.sin(jnp.pi * multiple.astype(jnp.float32) / (length + 1))

def eigen_values(length):
    counter = (jnp.arange(length, dtype=jnp.int32) + 1).astype(jnp.float32)
    return 2.0 - 2.0 * jnp.cos(jnp.pi * counter / (length + 1))

def interp_table(fine_start, fine_count, coarse_start, coarse_count, ratio):
    fine_pos = jnp.arange(fine_count, dtype=jnp.int32) + fine_start
    coarse_pos = jnp.arange(coarse_count, dtype=jnp.int32) + coarse_start
    numerator = 2 * fine_pos - (ratio - 1)
    lower_index = numerator // (2 * ratio)
    weight = ((numerator - 2 * ratio * lower_index).astype(jnp.float32) / (2 * ratio))[:, None]
    below = (coarse_pos[None, :] == lower_index[:, None]).astype(jnp.float32)
    above = (coarse_pos[None, :] == lower_index[:, None] + 1).astype(jnp.float32)
    return below * (1.0 - weight) + above * weight

def legendre_basis(length, count):
    points = (2.0 * jnp.arange(length, dtype=jnp.int32).astype(jnp.float32) + 1.0) / length - 1.0
    columns = [jnp.ones_like(points), points]
    for degree in range(2, count):
        columns.append(((2 * degree - 1) * points * columns[-1] - (degree - 1) * columns[-2]) / degree)
    columns = columns[:count]
    result = []
    for column in columns:
        vector = column
        for passes in range(2):
            for earlier in result:
                vector = vector - jnp.sum(earlier * vector) * earlier
        vector = vector / jnp.sqrt(jnp.sum(vector * vector))
        result.append(vector)
    return jnp.stack(result, axis=1)

def along_three(volume, first_table, second_table, third_table):
    volume = jnp.einsum('ai,ijk->ajk', first_table, volume, precision=highest)
    volume = jnp.einsum('bj,ijk->ibk', second_table, volume, precision=highest)
    return jnp.einsum('ck,ijk->ijc', third_table, volume, precision=highest)

def box_solve(patch):
    length = patch.shape[0] + 2 * W
    padded = jnp.pad(patch, W)
    table = sine_table(length)
    values = eigen_values(length)
    spectrum = along_three(padded, table, table, table)
    spectrum = spectrum / (values[:, None, None] + values[None, :, None] + values[None, None, :])
    return along_three(spectrum, table, table, table) * (2.0 / (length + 1)) ** 3

def coarse_charge(local):
    blocks = local.shape[0] // Q
    samples = local.reshape(blocks, Q, blocks, Q, blocks, Q).mean(axis=(1, 3, 5))
    padded = jnp.pad(samples, 1)
    beside = padded[2:, 1:-1, 1:-1] + padded[:-2, 1:-1, 1:-1]
    beside = beside + padded[1:-1, 2:, 1:-1] + padded[1:-1, :-2, 1:-1]
    beside = beside + padded[1:-1, 1:-1, 2:] + padded[1:-1, 1:-1, :-2]
    return (samples, (6.0 * samples - beside) / (Q * Q))

def face_planes(local, samples):
    length = local.shape[0]
    inner = length - 2 * W
    fine_table = interp_table(0, length, 0, samples.shape[0], Q)
    middle = fine_table[W:W + inner]

    def across_x(index):
        coarse_plane = jnp.einsum('j,jkl->kl', fine_table[index], samples, precision=highest)
        return local[index, W:W + inner, W:W + inner] - product(product(middle, coarse_plane), middle.T)

    def across_y(index):
        coarse_plane = jnp.einsum('k,jkl->jl', fine_table[index], samples, precision=highest)
        return local[W:W + inner, index, W:W + inner] - product(product(middle, coarse_plane), middle.T)
    own = jnp.stack([across_x(W - 1), across_x(W + inner), across_y(W - 1), across_y(W + inner)])
    outgoing = jnp.stack([across_x(W), across_x(W + inner - 1), across_y(W), across_y(W + inner - 1)])
    return (own, outgoing)

def coefficients(planes, basis):
    return jnp.einsum('ia,nij,jb->nab', basis, planes, basis, precision=highest)

def expand(coefs, basis):
    return jnp.einsum('ia,nab,jb->nij', basis, coefs, basis, precision=highest)

def coarse_faces(block, inner):
    cells = block.shape[2]
    edge = interp_table(-1, inner + 2, -1, cells + 2, Q)
    depth = interp_table(0, inner, 0, cells, Q)
    lateral = edge[1:inner + 1]

    def spread(plane):
        return product(product(lateral, plane), depth.T)
    return jnp.stack([spread(jnp.einsum('e,efk->fk', edge[0], block, precision=highest)), spread(jnp.einsum('e,efk->fk', edge[inner + 1], block, precision=highest)), spread(jnp.einsum('f,efk->ek', edge[0], block, precision=highest)), spread(jnp.einsum('f,efk->ek', edge[inner + 1], block, precision=highest))])

def dirichlet_solve(patch, faces):
    inner = patch.shape[0]
    source = patch.at[0].add(faces[0]).at[inner - 1].add(faces[1])
    source = source.at[:, 0].add(faces[2]).at[:, inner - 1].add(faces[3])
    table = sine_table(inner)
    values = eigen_values(inner)
    spectrum = along_three(source, table, table, table)
    spectrum = spectrum / (values[:, None, None] + values[None, :, None] + values[None, None, :])
    return along_three(spectrum, table, table, table) * (2.0 / (inner + 1)) ** 3

def coarse_solve(source):
    size_x, size_y, size_z = source.shape
    table_x = sine_table(size_x)
    table_y = sine_table(size_y)
    table_z = sine_table(size_z)
    values_x = eigen_values(size_x)
    values_y = eigen_values(size_y)
    values_z = eigen_values(size_z)
    spectrum = along_three(source, table_x, table_y, table_z)
    spectrum = spectrum * (Q * Q) / (values_x[:, None, None] + values_y[None, :, None] + values_z[None, None, :])
    scale = 2.0 / (size_x + 1) * (2.0 / (size_y + 1)) * (2.0 / (size_z + 1))
    return along_three(spectrum, table_x, table_y, table_z) * scale

def reference(charge):
    inner = P_SIZE
    cells = inner // Q
    margin_coarse = W // Q
    count = N_GX * N_GY
    patches = charge.reshape(N_GX, inner, N_GY, inner, inner).transpose(0, 2, 1, 3, 4).reshape(count, inner, inner, inner)
    basis = legendre_basis(inner, NL)

    def first_pass(patch):
        local = box_solve(patch)
        samples, spill = coarse_charge(local)
        own, outgoing = face_planes(local, samples)
        return (spill[:, :, margin_coarse:margin_coarse + cells], coefficients(own, basis), coefficients(outgoing, basis))
    spills, own_coefs, sent_coefs = lax.map(first_pass, patches)
    span = spills.shape[1]
    total = jnp.zeros((N_GX * cells + 2 * margin_coarse, N_GY * cells + 2 * margin_coarse, cells), jnp.float32)

    def deposit(index, total):
        index = index.astype(jnp.int32)
        start_x = (index // N_GY * cells).astype(jnp.int32)
        start_y = (index % N_GY * cells).astype(jnp.int32)
        anchor = jnp.zeros((), jnp.int32)
        current = lax.dynamic_slice(total, (start_x, start_y, anchor), (span, span, cells))
        return lax.dynamic_update_slice(total, current + spills[index], (start_x, start_y, anchor))
    total = lax.fori_loop(0, count, deposit, total)
    source = total[margin_coarse:margin_coarse + N_GX * cells, margin_coarse:margin_coarse + N_GY * cells]
    coarse = coarse_solve(source)
    rimmed = jnp.pad(coarse, ((1, 1), (1, 1), (0, 0)))
    grid_sent = sent_coefs.reshape(N_GX, N_GY, 4, NL, NL)
    no_pad = (0, 0)
    from_left = jnp.pad(grid_sent[:, :, 1], ((1, 0), no_pad, no_pad, no_pad))[:-1]
    from_right = jnp.pad(grid_sent[:, :, 0], ((0, 1), no_pad, no_pad, no_pad))[1:]
    from_below = jnp.pad(grid_sent[:, :, 3], (no_pad, (1, 0), no_pad, no_pad))[:, :-1]
    from_above = jnp.pad(grid_sent[:, :, 2], (no_pad, (0, 1), no_pad, no_pad))[:, 1:]
    received = jnp.stack([from_left, from_right, from_below, from_above], axis=2).reshape(count, 4, NL, NL)

    def second_pass(items):
        patch, own, incoming, index = items
        start_x = (index // N_GY * cells).astype(jnp.int32)
        start_y = (index % N_GY * cells).astype(jnp.int32)
        anchor = jnp.zeros((), jnp.int32)
        block = lax.dynamic_slice(rimmed, (start_x, start_y, anchor), (cells + 2, cells + 2, cells))
        faces = coarse_faces(block, inner) + expand(own + incoming, basis)
        return dirichlet_solve(patch, faces)
    solved = lax.map(second_pass, (patches, own_coefs, received, jnp.arange(count, dtype=jnp.int32)))
    return solved.reshape(N_GX, N_GY, inner, inner, inner).transpose(0, 2, 1, 3, 4).reshape(charge.shape)
```

```python
import functools

import jax
import jax.numpy as jnp
import ml_dtypes
import numpy as np
from jax import lax
from jax.experimental import pallas as pl
from jax.experimental.pallas import tpu as pltpu
from jax.sharding import PartitionSpec as P

P_SIZE = 32
W = 16
Q = 4
NL = 16
CLASSES = [(0, 0), (0, 1), (1, 0), (1, 1)]
MESH = pl.DeviceIdType.MESH


def sine_table(length):
    counter = np.arange(length) + 1
    return np.sin(np.pi * np.outer(counter, counter) / (length + 1))


def eigen_values(length):
    return 2.0 - 2.0 * np.cos(np.pi * (np.arange(length) + 1) / (length + 1))


def interp_table(fine_start, fine_count, coarse_start, coarse_count, ratio):
    fine_pos = np.arange(fine_count) + fine_start
    coarse_pos = np.arange(coarse_count) + coarse_start
    numerator = 2 * fine_pos - (ratio - 1)
    lower = numerator // (2 * ratio)
    weight = ((numerator - 2 * ratio * lower) / (2 * ratio))[:, None]
    below = coarse_pos[None, :] == lower[:, None]
    above = coarse_pos[None, :] == lower[:, None] + 1
    return below * (1.0 - weight) + above * weight


def legendre_basis(length, count):
    points = (2.0 * np.arange(length) + 1.0) / length - 1.0
    columns = [np.ones_like(points), points]
    for degree in range(2, count):
        columns.append(
            ((2 * degree - 1) * points * columns[-1] - (degree - 1) * columns[-2]) / degree
        )
    result = []
    for vector in columns[:count]:
        for passes in range(2):
            for earlier in result:
                vector = vector - np.sum(earlier * vector) * earlier
        result.append(vector / np.sqrt(np.sum(vector * vector)))
    return np.stack(result, axis=1)


def fold(length):
    half = length // 2
    eye = np.eye(length)
    return np.concatenate([eye[:half] + eye[::-1][:half], eye[:half] - eye[::-1][:half]])


def split(table):
    high = table.astype(ml_dtypes.bfloat16)
    low = (table - high.astype(np.float64)).astype(ml_dtypes.bfloat16)
    return high, low


def pack(blocks):
    parts, places, row = [], {}, 0
    for name, block in blocks.items():
        rows = -(-block.shape[0] // 16) * 16
        part = np.zeros((rows, 128), np.float32)
        part[: block.shape[0], : block.shape[1]] = block
        parts.append(part)
        places[name] = (row, rows, block.shape[1])
        row += rows
    return np.concatenate(parts), places


@functools.lru_cache(maxsize=None)
def tables(n_gx, n_gy):
    n, length, cells = P_SIZE, P_SIZE + 2 * W, P_SIZE // Q
    blocks, margin = length // Q, W // Q
    half, hl, hb, hn = n // 2, length // 2, blocks // 2, NL // 2
    nx, ny, nz = n_gx * cells, n_gy * cells, cells
    modes = ny * nz
    s_l, s_n = sine_table(length), sine_table(n)
    u_n, u_b = fold(n), fold(blocks)
    basis = legendre_basis(n, NL)
    average = np.kron(np.eye(blocks), np.full((1, Q), 1.0 / Q))
    fine = interp_table(0, length, 0, blocks, Q)
    middle = fine[W : W + n]
    picks = [W - 1, W, W + n - 1, W + n]

    big = {}
    big["fold"] = np.concatenate(
        [np.kron(u_n[p * half : (p + 1) * half], u_n[q * half : (q + 1) * half]) for p, q in CLASSES]
    ).T
    inner = s_l[:, W : W + n] @ u_n.T / 2
    f1 = [inner[p::2, p * half : (p + 1) * half] for p in (0, 1)]
    big["fwd"] = np.stack([np.kron(f1[p], f1[q]).T for p, q in CLASSES])
    a_full = average @ s_l
    b_full = basis.T @ s_l[W : W + n]
    a1 = [(u_b @ a_full)[p * hb : (p + 1) * hb, p::2] for p in (0, 1)]
    b1 = [b_full[p::2, p::2] for p in (0, 1)]
    back = []
    for p, q in CLASSES:
        part = np.zeros((hl * hl, 256))
        part[:, 0:64] = np.kron(a1[p], a1[q]).T
        part[:, 64:128] = np.kron(b1[p], b1[q]).T
        part[:, 128:192] = np.kron(s_l[picks][:, p::2], b_full[:, q::2]).T
        back.append(part)
    big["back"] = np.stack(back)

    unfold = u_b.T / 2
    pair = np.kron(unfold, unfold).reshape(blocks * blocks, 2, hb, 2, hb)

    def from_samples(table):
        folded = np.einsum("os,spaqb->pqabo", table, pair)
        out = np.zeros((4, 128, table.shape[0]))
        for c, (p, q) in enumerate(CLASSES):
            out[c, :64] = folded[p, q].reshape(hb * hb, -1)
        return out.reshape(512, -1)

    bm = basis.T @ middle
    lin_x = from_samples(np.kron(bm, bm)).reshape(512, NL, NL)
    lin = np.zeros((512, 640))
    for c, (p, q) in enumerate(CLASSES):
        lin[:, c * 128 + 64 : c * 128 + 128] = lin_x[:, p::2, q::2].reshape(512, hn * hn)
    lin[:, 512:576] = from_samples(np.kron(fine[picks], bm))
    big["lin"] = lin
    k1 = [(s_n @ u_n.T / 2)[p::2, p * half : (p + 1) * half] for p in (0, 1)]
    big["near"] = np.stack([np.kron(k1[p], k1[q]).T for p, q in CLASSES])
    r1 = [(u_n @ s_n / 2)[p * half : (p + 1) * half, p::2] for p in (0, 1)]
    big["far"] = np.stack([np.kron(r1[p], r1[q]).T for p, q in CLASSES])

    second = 2 * np.eye(blocks) - np.eye(blocks, k=1) - np.eye(blocks, k=-1)
    s_y, s_z = sine_table(ny), sine_table(nz)
    proj_z = np.zeros((nz, blocks))
    proj_z[:, margin : margin + cells] = s_z
    spread, drop = [], []
    edge = interp_table(-1, n + 2, -1, cells + 2, Q)
    depth = interp_table(0, n, 0, cells, Q)
    lateral = edge[1 : n + 1]
    s_ext = np.zeros((ny + 2, ny))
    s_ext[1:-1] = s_y
    sp = np.concatenate([s_n[0::2], s_n[1::2]])
    deep = sp @ depth @ s_z

    def by_class(first, second_table):
        parts = []
        for p, q in CLASSES:
            parts.append(
                np.kron(first[p * half : (p + 1) * half], second_table[q * half : (q + 1) * half])
            )
        return np.concatenate(parts).T

    factor = (2.0 / (ny + 1)) * (2.0 / (nz + 1))
    for b in range(n_gy):
        proj_y = np.zeros((ny, blocks))
        for j in range(blocks):
            at = j + b * cells - margin
            if 0 <= at < ny:
                proj_y[:, j] = s_y[:, at]
        plain = np.kron(proj_y, proj_z)
        curved = np.kron(proj_y @ second, proj_z) + np.kron(proj_y, proj_z @ second)
        spread.append(
            factor * np.concatenate([from_samples(curved), from_samples(plain)])
        )
        local_s = s_ext[b * cells : b * cells + cells + 2]
        rim = np.outer(sp[:, 0], edge[0] @ local_s) + np.outer(sp[:, n - 1], edge[n + 1] @ local_s)
        drop.append(
            np.concatenate([by_class(sp @ lateral @ local_s, deep), by_class(rim, deep)])
        )
    big["spread"] = np.stack(spread)
    big["drop"] = np.stack(drop)
    sb = s_n @ basis
    sbp = np.concatenate([sb[0::2], sb[1::2]])
    wcx = np.zeros((512, n * n))
    for c, (p, q) in enumerate(CLASSES):
        wcx[c * 128 + 64 : c * 128 + 128, c * 256 : c * 256 + 256] = np.kron(
            sb[p::2, p::2], sb[q::2, q::2]
        ).T
    big["facex"] = wcx
    ends = np.stack([sp[:, 0], sp[:, n - 1], sp[:, 0], sp[:, n - 1]], axis=1)
    wcy = np.zeros((128, n * n))
    wcy[:64] = by_class(ends, sbp)
    big["facey"] = wcy

    mu_y, mu_z = eigen_values(ny), eigen_values(nz)
    theta = np.arccosh(1.0 + (mu_y[:, None] + mu_z[None, :]).reshape(1, modes) / 2)
    below = 2 * np.sinh(theta) * (1.0 - np.exp(-2 * theta * (nx + 1)))
    rows = 2 * nx + 16
    apart = np.abs(np.arange(rows) - nx)[:, None]
    toep = (np.exp(-theta * apart) + np.exp(-theta * np.maximum(2 * (nx + 1) - apart, 0))) / below
    total = (np.arange(rows) - 1)[:, None]
    hank = (np.exp(-theta * (total + 2)) + np.exp(-theta * np.maximum(2 * nx - total, 0))) / below
    green = np.stack([toep, hank]).astype(np.float32)
    green = green.reshape(2, rows, modes // 128, 128).transpose(0, 2, 1, 3)

    mu_l, mu_n = eigen_values(length), eigen_values(n)
    sums = np.ones((8, 4 * hl * hl), np.float32)
    sums[0] = np.concatenate(
        [(mu_l[p::2][:, None] + mu_l[q::2][None, :]).ravel() for p, q in CLASSES]
    )
    sums[1, : n * n] = np.concatenate(
        [(mu_n[p::2][:, None] + mu_n[q::2][None, :]).ravel() for p, q in CLASSES]
    )
    left = np.zeros((48, length))
    left[:16] = a_full
    left[16:20] = s_l[picks]
    left[32:48] = b_full
    flat = np.zeros((32, blocks))
    flat[:4] = fine[picks]
    flat[16:32] = bm
    u12 = np.zeros((64, 16))
    u12[:32, :10] = np.outer(s_n[:, 0], edge[0]) + np.outer(s_n[:, n - 1], edge[n + 1])
    u12[32:, :10] = s_n @ lateral
    lf = np.zeros((32, 24))
    lf[:, 0], lf[:, 3] = s_n[:, 0], s_n[:, n - 1]
    lf[:, 8 + 2] = s_n[:, 0]
    lf[:, 16 + 1] = s_n[:, n - 1]
    small, places = pack(
        {
            "sl": s_l[:, W : W + n],
            "left": left * (2.0 / (length + 1)) ** 3,
            "flat": flat,
            "second": second,
            "sn": s_n,
            "u12": u12,
            "lf": lf,
            "sb": sb,
            "mul": mu_l[:, None],
            "mun": mu_n[:, None],
        }
    )
    return big, green, sums, small, places


def halves(value):
    high = value.astype(jnp.bfloat16)
    return high, (value - high.astype(jnp.float32)).astype(jnp.bfloat16)


def mm(left, right):
    return jnp.dot(left, right, preferred_element_type=jnp.float32)


def right_mul(value, table):
    rows = value.shape[0]
    high, low = halves(value)
    both = mm(jnp.concatenate([high, low], axis=0), table[0])
    return both[:rows] + both[rows:] + mm(high, table[1])


def left_mul(table, value):
    rows = table.shape[0]
    th, tl = halves(table)
    vh, vl = halves(value)
    both = mm(jnp.concatenate([th, tl], axis=0), vh)
    return both[:rows] + both[rows:] + mm(th, vl)


NAMES = ["fold", "fwd", "back", "lin", "spread", "near", "facex", "facey", "drop", "far"]


def kernel(names, places, n_gx, n_gy, *refs):
    count = len(names)
    charge_ref, small_ref, sums_ref = refs[:3]
    hbm = dict(zip(names, refs[3 : 3 + count]))
    out_ref = refs[3 + count]
    vmem = dict(zip(names, refs[4 + count : 4 + 2 * count]))
    (pack_ref, cx_ref, cy_ref, all_ref, rx_ref, ry_ref, src_ref, load_sem, s_sem, r_sem, n_send, n_recv) = refs[
        4 + 2 * count :
    ]
    ndev = n_gx * n_gy
    a = lax.axis_index("gx")
    b = lax.axis_index("gy")
    me = a * n_gy + b
    n, cells = P_SIZE, P_SIZE // Q

    loads = {}
    for i, name in enumerate(names):
        source = hbm[name]
        if name[:-1] in ("spread", "drop"):
            source = source.at[b]
        loads[name] = pltpu.make_async_copy(source, vmem[name], load_sem.at[i])
        loads[name].start()

    barrier = pltpu.get_barrier_semaphore()

    def greet(r, carry):
        peer = lax.rem(me + r, ndev)
        pl.semaphore_signal(
            barrier, inc=1, device_id=(peer // n_gy, lax.rem(peer, n_gy)), device_id_type=MESH
        )
        return carry

    lax.fori_loop(1, ndev, greet, 0)

    def small(name):
        row, rows, cols = places[name]
        return small_ref[row : row + rows, 0:cols]

    def table(name, index=None):
        if index is None:
            return vmem[name + "0"][...], vmem[name + "1"][...]
        return vmem[name + "0"][index], vmem[name + "1"][index]

    def ready(*wanted):
        for name in wanted:
            loads[name].wait()

    charge = charge_ref[...]
    ready("fold0")
    folding = vmem["fold0"][...]
    high, low = halves(charge)
    both = mm(jnp.concatenate([high, low], axis=0), folding)
    folded = both[:n] + both[n:]
    wide = left_mul(small("sl"), folded)
    ready("fwd0", "fwd1", "back0", "back1")
    samples, cx = [], []
    cy = None
    for c in range(4):
        spectrum = right_mul(wide[:, c * 256 : (c + 1) * 256], table("fwd", c))
        spectrum = spectrum / (small("mul") + sums_ref[0:1, c * 1024 : (c + 1) * 1024])
        out = right_mul(left_mul(small("left"), spectrum), table("back", c))
        samples.append(out[0:16, 0:128])
        cx.append(out[16:32, 0:128])
        cy = out[32:48, 128:256] if cy is None else cy + out[32:48, 128:256]
    samples = jnp.concatenate(samples, axis=1)
    cx = jnp.concatenate(cx, axis=1)
    ready("spread0", "spread1")
    bent = left_mul(small("second"), samples)
    packet = right_mul(jnp.concatenate([samples, bent], axis=1), table("spread"))
    pack_ref[...] = packet

    pl.semaphore_wait(barrier, ndev - 1)

    def send(r):
        peer = lax.rem(me + r, ndev)
        return pltpu.make_async_remote_copy(
            src_ref=pack_ref,
            dst_ref=all_ref.at[me],
            send_sem=s_sem.at[r],
            recv_sem=r_sem.at[me],
            device_id=(peer // n_gy, lax.rem(peer, n_gy)),
            device_id_type=MESH,
        )

    def start(r, carry):
        send(r).start()
        return carry

    lax.fori_loop(1, ndev, start, 0)
    all_ref[me] = packet

    ready("lin0", "lin1")
    flat = right_mul(left_mul(small("flat"), samples), table("lin"))
    cx = cx - flat[0:16, 0:512]
    cy = cy - flat[16:32, 512:640]
    cx_ref[...] = cx[0:8]
    cy_ref[...] = cy
    right, left = lax.rem(a + 1, n_gx), lax.rem(a + n_gx - 1, n_gx)
    upper, lower = lax.rem(b + 1, n_gy), lax.rem(b + n_gy - 1, n_gy)
    near = []
    for i, (source, target, device) in enumerate(
        [
            (cx_ref, rx_ref.at[0], (right, b)),
            (cx_ref, rx_ref.at[1], (left, b)),
            (cy_ref, ry_ref.at[0], (a, upper)),
            (cy_ref, ry_ref.at[1], (a, lower)),
        ]
    ):
        copy = pltpu.make_async_remote_copy(
            src_ref=source,
            dst_ref=target,
            send_sem=n_send.at[i],
            recv_sem=n_recv.at[i],
            device_id=device,
            device_id_type=MESH,
        )
        copy.start()
        near.append(copy)

    ready("near0", "near1", "facex0", "facex1", "facey0", "facey1")
    narrow = left_mul(small("sn"), folded)
    spectrum = jnp.concatenate(
        [right_mul(narrow[:, c * 256 : (c + 1) * 256], table("near", c)) for c in range(4)], axis=1
    )

    for copy in near:
        copy.wait()
    from_left = jnp.where(a > 0, rx_ref[0], 0.0)
    from_right = jnp.where(a < n_gx - 1, rx_ref[1], 0.0)
    faces = jnp.concatenate([cx[0:8], from_left, from_right], axis=0)
    spectrum = spectrum + right_mul(left_mul(small("lf"), faces), table("facex"))
    group = lax.broadcasted_iota(jnp.int32, (16, 128), 1) // 16
    total = jnp.where((group == 0) | (group == 3), cy, 0.0)
    total = total + jnp.where((group == 2) & (b > 0), ry_ref[0], 0.0)
    total = total + jnp.where((group == 1) & (b < n_gy - 1), ry_ref[1], 0.0)
    spectrum = spectrum + right_mul(left_mul(small("sb"), total), table("facey"))

    def arrive(r, carry):
        origin = lax.rem(me + ndev - r, ndev)
        pltpu.make_async_remote_copy(
            src_ref=pack_ref,
            dst_ref=all_ref.at[origin],
            send_sem=s_sem.at[r],
            recv_sem=r_sem.at[origin],
            device_id=(origin // n_gy, lax.rem(origin, n_gy)),
            device_id_type=MESH,
        ).wait()
        return carry

    lax.fori_loop(1, ndev, arrive, 0)

    src_ref[...] = jnp.zeros_like(src_ref)

    def gather(k, carry):
        part = all_ref[k * n_gy]
        for j in range(1, n_gy):
            part = part + all_ref[k * n_gy + j]
        place = pl.ds(pl.multiple_of(k * cells, cells), 16)
        src_ref[place] = src_ref[place] + part
        return carry

    lax.fori_loop(0, n_gx, gather, 0)
    nx = n_gx * cells
    source = src_ref[4 : 4 + nx]
    ready("toep", "hank")
    values = []
    for i in range(cells + 2):
        row = []
        for g in range(source.shape[1] // 128):
            influence = (
                vmem["toep"][g, pl.ds(nx + 1 - i - a * cells, nx)]
                - vmem["hank"][g, pl.ds(a * cells + i, nx)]
            )
            part = influence * source[:, g * 128 : (g + 1) * 128]
            row.append(jnp.sum(part, axis=0, keepdims=True))
        values.append(jnp.concatenate(row, axis=1))
    values.append(jnp.zeros((16 - len(values), source.shape[1]), jnp.float32))
    coarse = jnp.concatenate(values, axis=0)
    ready("drop0", "drop1", "far0", "far1")
    lifted = left_mul(small("u12"), coarse)
    spectrum = spectrum + right_mul(
        jnp.concatenate([lifted[:n], lifted[n:]], axis=1), table("drop")
    )
    spectrum = spectrum * ((2.0 / (n + 1)) ** 3) / (small("mun") + sums_ref[1:2, 0 : n * n])
    spectrum = left_mul(small("sn"), spectrum)
    final = jnp.concatenate(
        [right_mul(spectrum[:, c * 256 : (c + 1) * 256], table("far", c)) for c in range(4)], axis=1
    )
    high, low = halves(final)
    both = lax.dot_general(
        jnp.concatenate([high, low], axis=0),
        folding,
        (((1,), (1,)), ((), ())),
        preferred_element_type=jnp.float32,
    )
    out_ref[...] = both[:n] + both[n:]


def body(n_gx, n_gy, charge):
    big, green, sums, small, places = tables(n_gx, n_gy)
    names, arrays = [], []
    for name in NAMES:
        if name == "fold":
            names.append("fold0")
            arrays.append(big[name].astype(ml_dtypes.bfloat16))
            continue
        for i, part in enumerate(split(big[name])):
            names.append(name + str(i))
            arrays.append(part)
    names += ["toep", "hank"]
    arrays += [green[0], green[1]]
    scratch = []
    for name, array in zip(names, arrays):
        shape = array.shape[1:] if name[:-1] in ("spread", "drop") else array.shape
        scratch.append(pltpu.VMEM(shape, array.dtype))
    ndev = n_gx * n_gy
    cells = P_SIZE // Q
    modes = n_gy * cells * cells
    scratch += [
        pltpu.VMEM((16, modes), jnp.float32),
        pltpu.VMEM((8, 512), jnp.float32),
        pltpu.VMEM((16, 128), jnp.float32),
        pltpu.VMEM((ndev, 16, modes), jnp.float32),
        pltpu.VMEM((2, 8, 512), jnp.float32),
        pltpu.VMEM((2, 16, 128), jnp.float32),
        pltpu.VMEM((n_gx * cells + 8, modes), jnp.float32),
        pltpu.SemaphoreType.DMA((len(names),)),
        pltpu.SemaphoreType.DMA((ndev,)),
        pltpu.SemaphoreType.DMA((ndev,)),
        pltpu.SemaphoreType.DMA((4,)),
        pltpu.SemaphoreType.DMA((4,)),
    ]
    vm = pl.BlockSpec(memory_space=pltpu.VMEM)
    return pl.pallas_call(
        functools.partial(kernel, names, places, n_gx, n_gy),
        out_shape=jax.ShapeDtypeStruct(charge.shape, charge.dtype),
        in_specs=[vm] * 3 + [pl.BlockSpec(memory_space=pl.ANY)] * len(names),
        out_specs=vm,
        scratch_shapes=scratch,
        name="mlc",
        compiler_params=pltpu.CompilerParams(
            collective_id=0, has_side_effects=True, vmem_limit_bytes=60 * 1024 * 1024
        ),
    )(charge, small, sums, *[jnp.asarray(array) for array in arrays])


def solution(mesh):
    run = functools.partial(body, mesh.shape["gx"], mesh.shape["gy"])
    spec = P("gx", "gy")
    return jax.shard_map(run, mesh=mesh, in_specs=(spec,), out_specs=spec, check_vma=False)
```
